512 devices in a mesh: dp: 32 (over y, z_lo), tensor: 16 (over z_hi, x, core).
Axes of the slice: x: 4, y: 8, z: 8 (z_hi: 2, z_lo: 4; z = z_hi * 4 + z_lo), core: 2. Of those that a mesh axis runs over, the one named last changes fastest.
Arguments:
- hidden: bfloat16 [24576, 14336], P('dp', 'tensor'), may hold values from -0.0390625 to 0.0390625
- out_grad: bfloat16 [24576, 8192], P(('dp', 'tensor')), may hold values from -6 to 6
- weights: bfloat16 [16, 32, 128, 128], P('tensor'), may hold values from -0.125 to 0.125
- block_rows: int32 [16, 32], P('tensor'), may hold values from 0 to 6, as said below
- block_cols: int32 [16, 32], P('tensor'), may hold values from 0 to 63, as said below
- counts: int32 [16], P('tensor'), may hold values from 16 to 32, as said below
Outputs:
- weight_grad: float32 [16, 32, 128, 128], P('tensor', 'dp')
- input_grad: bfloat16 [24576, 14336], P('dp', 'tensor')
The draws below stay inside these ranges and needn't reach their ends.
Inputs may be any that keep to these rules, and one draw needn't show every extreme that they name: `block_rows`: within one member, no two slots name the same pair of block row and block column. `block_cols`: pairs with block_rows as stated there. `counts`: some member has all 32 slots live.
All inputs are finite; a program needn't handle non-finite values.
Results may differ from the reference program's by a relative error of at most 0.001.
Values may be sent and summed in bfloat16 or wider, within the bound.
No kernel may reach another device: no remote copies, remote signals or barrier semaphores. Data moves between devices by JAX's collectives and lax.ppermute only.
A program may use at most 128 MiB of HBM per device.

```python
import jax
import jax.numpy as jnp
from jax import lax

D = 8192
FF = 14336
BLK = 128
SLOTS = 32
TOKENS = 24576
PANEL = 7
NBC = 64
N_TENSOR = 16


def block_cells(key):
    member_keys = jax.random.split(jax.random.fold_in(key, 11), N_TENSOR)
    orders = jax.vmap(lambda single: jax.random.permutation(single, PANEL * NBC))(member_keys)
    return orders[:, :SLOTS].astype(jnp.int32)


def draw_block_rows(key, part):
    return block_cells(key) // NBC


def draw_block_cols(key, part):
    return block_cells(key) % NBC


def draw_counts(key, part):
    values = jax.random.randint(jax.random.fold_in(key, 5), (N_TENSOR,), SLOTS // 2, SLOTS + 1)
    fullest = jax.random.randint(jax.random.fold_in(key, 6), (), 0, N_TENSOR)
    return values.at[fullest].set(SLOTS).astype(jnp.int32)


def block_scale(stream_key, extent, pieces, smallest, top_value):
    level = 1.0
    for dim, parts in pieces:
        heights = jax.random.uniform(jax.random.fold_in(jax.random.fold_in(stream_key, 6), dim), (parts,), jnp.float32, smallest / len(pieces), top_value / len(pieces))
        level = level * jnp.repeat(jnp.exp(heights), extent[dim] // parts).reshape((-1,) + (1,) * (len(extent) - 1 - dim))
    return level


def gaussian(key, shape, spread, bound, shards=(), held_as=jnp.bfloat16):
    gain = block_scale(key, shape, shards, -0.22, 0.18) if shards else 1.0
    result = jax.random.normal(key, shape, jnp.float32) * spread * gain
    return jnp.minimum(jnp.maximum(result, -bound), bound).astype(held_as)


def setup_inputs(seed: int = 0) -> dict:
    key_list = jax.random.split(jax.random.key(seed), 7)
    return {
        "hidden": gaussian(key_list[0], (TOKENS, FF), (TOKENS ** -0.5), 0.0390625, ((0, 32), (1, 16))),
        "out_grad": gaussian(key_list[1], (TOKENS, D), 1.0, 6.0, ((0, 512),)),
        "weights": gaussian(key_list[2], (N_TENSOR, SLOTS, BLK, BLK), (D // 4) ** -0.5, 0.125, ((0, 16),)),
        "block_rows": draw_block_rows(jax.random.fold_in(key_list[6], 71), 0),
        "block_cols": draw_block_cols(jax.random.fold_in(key_list[6], 71), 0),
        "counts": draw_counts(jax.random.fold_in(key_list[6], 71), 0),
    }


def member_terms(member, hidden, out_grad, weights, block_rows, block_cols, counts):
    width = hidden.shape[1] // N_TENSOR
    act_panel = lax.dynamic_slice_in_dim(hidden, member * width, width, 1)
    own_weights = weights[member]
    own_rows = block_rows[member]
    own_cols = block_cols[member]
    active_count = counts[member]

    def slot_step(running_totals, position_slot):
        starting_row = (own_rows[position_slot] * BLK).astype(jnp.int32)
        col_start = (own_cols[position_slot] * BLK).astype(jnp.int32)
        active_flags = (position_slot < active_count).astype(jnp.float32)
        activation_block = lax.dynamic_slice_in_dim(act_panel, starting_row, BLK, 1)
        gradient_block = lax.dynamic_slice_in_dim(out_grad, col_start, BLK, 1)
        block_gradient = jnp.dot(activation_block.T, gradient_block, preferred_element_type=jnp.float32) * active_flags
        contribution = jnp.dot(gradient_block, own_weights[position_slot].T, preferred_element_type=jnp.float32)
        preceding_count = lax.dynamic_slice_in_dim(running_totals, starting_row, BLK, 1)
        running_totals = lax.dynamic_update_slice_in_dim(running_totals, preceding_count + active_flags * contribution, starting_row, 1)
        return running_totals, block_gradient

    initial = jnp.zeros((hidden.shape[0], width), jnp.float32)
    running_totals, grads = lax.scan(slot_step, initial, jnp.arange(SLOTS, dtype=jnp.int32))
    return running_totals.astype(jnp.bfloat16), grads


def reference(hidden, out_grad, weights, block_rows, block_cols, counts):
    def one_member(member):
        return member_terms(member, hidden, out_grad, weights, block_rows, block_cols, counts)

    panels, weight_grad = lax.map(one_member, jnp.arange(N_TENSOR, dtype=jnp.int32))
    input_grad = jnp.transpose(panels, (1, 0, 2)).reshape(hidden.shape[0], hidden.shape[1])
    return weight_grad, input_grad
```

```python
import functools

import jax
import jax.numpy as jnp
from jax import lax
from jax.experimental import pallas as pl
from jax.experimental.pallas import tpu as pltpu
from jax.sharding import PartitionSpec as P

BLK = 128
X = 4
MEMBERS = 4 * X
HALF = 2 * X


def swap_half(i):
    return i ^ HALF


def swap_core(i):
    return i ^ 1


def along_x(step):
    def move(i):
        return (i // HALF) * HALF + ((i // 2 + step) % X) * 2 + i % 2

    return move


def send(value, target):
    return lax.ppermute(value, "tensor", [(i, target(i)) for i in range(MEMBERS)])


def grads_kernel(has_prior, half_ref, rows_ref, cols_ref, offs_ref, *refs):
    pieces = refs[:HALF]
    hidden_ref, weights_ref = refs[HALF : HALF + 2]
    if has_prior:
        prior_ref = refs[HALF + 2]
    weight_grad_ref, input_grad_ref, total = refs[-3:]
    height = pieces[0].shape[0]
    offs = [pl.multiple_of(offs_ref[i], 16) for i in range(HALF)]
    total[...] = jnp.zeros_like(total)
    nothing = jnp.zeros((BLK, BLK), weights_ref.dtype)

    def pair_step(pair, carry):
        slots = (2 * pair, 2 * pair + 1)
        rows = [pl.ds(pl.multiple_of(rows_ref[s] * BLK, BLK), BLK) for s in slots]
        cols = [pl.ds(pl.multiple_of(cols_ref[s] * BLK, BLK), BLK) for s in slots]
        grad = jnp.concatenate(
            [jnp.concatenate([piece[:, c] for piece in pieces], 0) for c in cols], 1
        )
        act = jnp.concatenate(
            [jnp.concatenate([hidden_ref[pl.ds(o, height), r] for o in offs], 0) for r in rows], 1
        )
        w0, w1 = weights_ref[slots[0]], weights_ref[slots[1]]
        both = jnp.concatenate(
            [jnp.concatenate([w0, nothing], 1), jnp.concatenate([nothing, w1], 1)], 0
        )
        blocks = lax.dot_general(
            act, grad, (((0,), (0,)), ((), ())), preferred_element_type=jnp.float32
        )
        moved = lax.dot_general(
            grad, both, (((1,), (1,)), ((), ())), preferred_element_type=jnp.float32
        )
        for k, s in enumerate(slots):
            part = slice(k * BLK, (k + 1) * BLK)
            block = blocks[part, part]
            if has_prior:
                block = block + prior_ref[s]
            weight_grad_ref[s] = block
            total[:, rows[k]] += moved[:, part]
        return carry

    lax.fori_loop(0, weights_ref.shape[0] // 2, pair_step, 0)
    for i, o in enumerate(offs):
        input_grad_ref[pl.ds(o, height), :] = total[i * height : (i + 1) * height, :].astype(
            input_grad_ref.dtype
        )


def half_grads(pieces, half, offs, rows, cols, hidden, weights, prior):
    height, width = pieces[0].shape
    slots = weights.shape[0]
    panel = hidden.shape[1]
    tall = HALF * height
    whole2 = lambda i, *_: (0, 0)
    whole3 = lambda i, *_: (0, 0, 0)
    at_half = lambda i, half_ref, *_: (half_ref[0], 0)
    one = pl.Buffered(1)
    in_specs = [pl.BlockSpec((height, width), whole2, pipeline_mode=one) for _ in pieces]
    in_specs += [
        pl.BlockSpec((tall, panel), at_half, pipeline_mode=one),
        pl.BlockSpec(weights.shape, whole3, pipeline_mode=one),
    ]
    operands = [half[None], rows, cols, offs, *pieces, hidden, weights]
    aliases = {}
    if prior is not None:
        in_specs += [
            pl.BlockSpec((slots, BLK, BLK), whole3, pipeline_mode=one),
            pl.BlockSpec(memory_space=pl.ANY),
        ]
        aliases = {len(operands) + 1: 1}
        operands += list(prior)
    moved = 2 * tall * width + 2 * tall * panel * 2 + 6 * slots * BLK * BLK
    return pl.pallas_call(
        functools.partial(grads_kernel, prior is not None),
        grid_spec=pltpu.PrefetchScalarGridSpec(
            num_scalar_prefetch=4,
            grid=(1,),
            in_specs=in_specs,
            out_specs=[
                pl.BlockSpec((slots, BLK, BLK), whole3, pipeline_mode=one),
                pl.BlockSpec((tall, panel), at_half, pipeline_mode=one),
            ],
            scratch_shapes=[pltpu.VMEM((tall, panel), jnp.float32)],
        ),
        out_shape=[
            jax.ShapeDtypeStruct((slots, BLK, BLK), jnp.float32),
            jax.ShapeDtypeStruct(hidden.shape, hidden.dtype),
        ],
        input_output_aliases=aliases,
        compiler_params=pltpu.CompilerParams(vmem_limit_bytes=24 * 2**20),
        cost_estimate=pl.CostEstimate(
            flops=8 * slots * tall * BLK * BLK, bytes_accessed=moved, transcendentals=0
        ),
    )(*operands)


def shards(hidden, out_grad, weights, block_rows, block_cols, counts):
    height = out_grad.shape[0]
    slots = weights.shape[1]
    rows, cols = block_rows[0], block_cols[0]
    live = jnp.arange(slots, dtype=jnp.int32) < counts[0]
    masked = jnp.where(live[:, None, None], weights[0], jnp.zeros((), weights.dtype))
    me = lax.axis_index("tensor")
    half, x, core = me // HALF, (me // 2) % X, me % 2

    other = send(out_grad, swap_half)
    steps = (1, X - 1, 2)
    near = [out_grad] + [send(out_grad, along_x(k)) for k in steps]
    far = [other] + [send(other, along_x(k)) for k in steps]
    home = [(x - k) % X for k in (0, *steps)]
    offs = jnp.stack(
        [(p * 2 + core) * height for p in home] + [(p * 2 + 1 - core) * height for p in home]
    )
    near_all = near + [send(v, swap_core) for v in near]
    far_all = far + [send(v, swap_core) for v in far]

    first = half_grads(near_all, half, offs, rows, cols, hidden, masked, None)
    weight_sum, input_grad = half_grads(far_all, 1 - half, offs, rows, cols, hidden, masked, first)

    share = slots // lax.axis_size("dp")
    parts = lax.all_to_all(weight_sum, "dp", split_axis=0, concat_axis=0, tiled=True)
    summed = parts.reshape(-1, share, BLK, BLK).sum(0)
    mine = lax.axis_index("dp") * share + jnp.arange(share, dtype=jnp.int32)
    summed = jnp.where((mine < counts[0])[:, None, None], summed, 0.0)
    return summed[None], input_grad


def solution(mesh):
    in_specs = (
        P("dp", "tensor"),
        P(("dp", "tensor"), None),
        P("tensor", None, None, None),
        P("tensor", None),
        P("tensor", None),
        P("tensor"),
    )
    out_specs = (P("tensor", "dp", None, None), P("dp", "tensor"))
    return jax.shard_map(shards, mesh=mesh, in_specs=in_specs, out_specs=out_specs, check_vma=False)
```

```python
import functools

import jax
import jax.numpy as jnp
from jax import lax
from jax.experimental import pallas as pl
from jax.experimental.pallas import tpu as pltpu
from jax.sharding import PartitionSpec as P


BLK = 128
EXTRA = 8
SHIFT = 14.0
TINY = 1e-30
X = 4
MEMBERS = 4 * X
HALF = 2 * X


def swap_half(i):
    return i ^ HALF


def swap_core(i):
    return i ^ 1


def along_x(step):
    def move(i):
        return (i // HALF) * HALF + ((i // 2 + step) % X) * 2 + i % 2

    return move


def send(value, target):
    return lax.ppermute(value, "tensor", [(i, target(i)) for i in range(MEMBERS)])


def gather_rows(pieces, cols):
    return jnp.concatenate(
        [jnp.concatenate([piece[:, c] for piece in pieces], 0) for c in cols], 1
    )


def blocks_of(table_ref, slots):
    return [pl.ds(pl.multiple_of(table_ref[s] * BLK, BLK), BLK) for s in slots]


def weight_kernel(count, first, coded, rows_ref, cols_ref, offs_ref, *refs):
    pieces, hidden_ref, out_ref = refs[:count], refs[count], refs[-1]
    height = pieces[0].shape[0]
    offs = [pl.multiple_of(offs_ref[first + i], 16) for i in range(count)]

    def pair_step(pair, carry):
        slots = (2 * pair, 2 * pair + 1)
        grad = gather_rows(pieces, blocks_of(cols_ref, slots))
        act = jnp.concatenate(
            [
                jnp.concatenate([hidden_ref[pl.ds(o, height), r] for o in offs], 0)
                for r in blocks_of(rows_ref, slots)
            ],
            1,
        )
        blocks = lax.dot_general(
            act, grad, (((0,), (0,)), ((), ())), preferred_element_type=jnp.float32
        )
        for k, s in enumerate(slots):
            block = blocks[k * BLK : (k + 1) * BLK, k * BLK : (k + 1) * BLK]
            if coded:
                block = block + refs[count + 1][s]
                top = jnp.max(jnp.abs(block), axis=0, keepdims=True)
                power = jnp.ceil(jnp.log2(jnp.maximum(top, TINY)))
                out_ref[s, :BLK, :] = block * jnp.exp2(SHIFT - power)
                out_ref[s, BLK:, :] = jnp.broadcast_to(power, (EXTRA, BLK))
            else:
                out_ref[s] = block
        return carry

    lax.fori_loop(0, rows_ref.shape[0] // 2, pair_step, 0)


def input_kernel(count, rows_ref, cols_ref, offs_ref, counts_ref, *refs):
    pieces, (weights_ref, out_ref, total) = refs[:count], refs[count:]
    height = pieces[0].shape[0]
    total[...] = jnp.zeros_like(total)
    nothing = jnp.zeros((BLK, BLK), weights_ref.dtype)

    def pair_step(pair, carry):
        slots = (2 * pair, 2 * pair + 1)
        grad = gather_rows(pieces, blocks_of(cols_ref, slots))
        w = []
        for s in slots:
            live = (s < counts_ref[0]).astype(jnp.float32)
            w.append((weights_ref[s].astype(jnp.float32) * live).astype(weights_ref.dtype))
        both = jnp.concatenate(
            [jnp.concatenate([w[0], nothing], 1), jnp.concatenate([nothing, w[1]], 1)], 0
        )
        moved = lax.dot_general(
            grad, both, (((1,), (1,)), ((), ())), preferred_element_type=jnp.float32
        )
        for k, r in enumerate(blocks_of(rows_ref, slots)):
            total[:, r] += moved[:, k * BLK : (k + 1) * BLK]
        return carry

    lax.fori_loop(0, rows_ref.shape[0] // 2, pair_step, 0)
    for i in range(count):
        o = pl.multiple_of(offs_ref[i], 16)
        out_ref[pl.ds(o, height), :] = total[i * height : (i + 1) * height, :].astype(out_ref.dtype)


def staged(kernel, n_tables, n_in, out_staged, *refs):
    tables, sources, out_ref = refs[:n_tables], refs[n_tables : n_tables + n_in], refs[n_tables + n_in]
    sems, *held = refs[n_tables + n_in + 1 :]
    held, extra = held[:n_in], held[n_in:]
    copies = [pltpu.make_async_copy(sources[i], held[i], sems.at[i]) for i in range(n_in)]
    for copy in copies:
        copy.start()
    for copy in copies:
        copy.wait()
    if not out_staged:
        kernel(*tables, *held, out_ref, *extra)
        return
    kernel(*tables, *held, extra[0], *extra[1:])
    copy = pltpu.make_async_copy(extra[0], out_ref, sems.at[n_in])
    copy.start()
    copy.wait()


def call(kernel, tables, operands, out, scratch, flops, out_staged=False):
    far = pl.BlockSpec(memory_space=pltpu.HBM)
    zeros = (0,) * len(out.shape)
    near = pl.BlockSpec(out.shape, lambda i, *_: zeros, pipeline_mode=pl.Buffered(1))
    size = sum(v.size * v.dtype.itemsize for v in (*operands, out))
    held = [pltpu.VMEM(v.shape, v.dtype) for v in operands + ((out,) if out_staged else ())]
    return pl.pallas_call(
        functools.partial(staged, kernel, len(tables), len(operands), out_staged),
        grid_spec=pltpu.PrefetchScalarGridSpec(
            num_scalar_prefetch=len(tables),
            grid=(1,),
            in_specs=[far for _ in operands],
            out_specs=far if out_staged else near,
            scratch_shapes=[pltpu.SemaphoreType.DMA((len(operands) + 1,)), *held, *scratch],
        ),
        out_shape=out,
        compiler_params=pltpu.CompilerParams(vmem_limit_bytes=GRANT),
        cost_estimate=pl.CostEstimate(flops=flops, bytes_accessed=size, transcendentals=0),
    )(*tables, *operands)


def weight_grads(pieces, first, tables, hidden, slots, prior=None):
    coded = prior is not None
    kernel = functools.partial(weight_kernel, len(pieces), first, coded)
    out = jax.ShapeDtypeStruct((slots, BLK + EXTRA * coded, BLK), jnp.float32)
    operands = (*pieces, hidden) + ((prior,) if coded else ())
    flops = 4 * slots * len(pieces) * pieces[0].shape[0] * BLK * BLK
    return call(kernel, tables, operands, out, [], flops, out_staged=not coded)


def input_grads(pieces, tables, weights, like):
    kernel = functools.partial(input_kernel, len(pieces))
    out = jax.ShapeDtypeStruct(like.shape, like.dtype)
    flops = 4 * weights.shape[0] * like.shape[0] * BLK * BLK
    scratch = [pltpu.VMEM(like.shape, jnp.float32)]
    return call(kernel, tables, (*pieces, weights), out, scratch, flops)


def shards(hidden, out_grad, weights, block_rows, block_cols, counts):
    return body(hidden, out_grad, weights[0], block_rows[0], block_cols[0], counts)


def body(hidden, out_grad, weights, rows, cols, counts):
    height = out_grad.shape[0]
    slots = weights.shape[0]
    me = lax.axis_index("tensor")
    half, x, core = me // HALF, (me // 2) % X, me % 2

    other = send(out_grad, swap_half)
    near = [out_grad] + [send(out_grad, along_x(k)) for k in STEPS[1:]]
    far = [other] + [send(other, along_x(k)) for k in STEPS[1:]]
    pieces, places = [], []
    for shards_, h in ((near, half), (far, 1 - half)):
        for k, shard in zip(STEPS, shards_):
            chip = h * HALF + (x - k) % X * 2
            pieces += [shard, send(shard, swap_core)]
            places += [(chip + core) * height, (chip + 1 - core) * height]
    tables = (rows, cols, jnp.stack(places))

    prior = weight_grads(pieces[:EARLY], 0, tables, hidden, slots)
    coded = weight_grads(pieces[EARLY:], EARLY, tables, hidden, slots, prior)
    parts = lax.all_to_all(coded.astype(jnp.float16), "dp", split_axis=0, concat_axis=0, tiled=True)
    input_grad = input_grads(pieces, (*tables, counts), weights, hidden)

    share = slots // lax.axis_size("dp")
    parts = parts.astype(jnp.float32).reshape(-1, share, BLK + EXTRA, BLK)
    summed = (parts[:, :, :BLK] * jnp.exp2(parts[:, :, BLK : BLK + 1] - SHIFT)).sum(0)
    mine = lax.axis_index("dp") * share + jnp.arange(share, dtype=jnp.int32)
    summed = jnp.where((mine < counts[0])[:, None, None], summed, 0.0)
    return summed[None], input_grad


STEPS = (0, 1, X - 1, 2)
EARLY = 2 * X + 2
GRANT = 60 * 2**20


def solution(mesh):
    in_specs = (
        P("dp", "tensor"),
        P(("dp", "tensor"), None),
        P("tensor", None, None, None),
        P("tensor", None),
        P("tensor", None),
        P("tensor"),
    )
    out_specs = (P("tensor", "dp", None, None), P("dp", "tensor"))
    return jax.shard_map(
        shards, mesh=mesh, in_specs=in_specs, out_specs=out_specs, check_vma=False
    )
```

```python
import functools

import jax
import jax.numpy as jnp
from jax import lax
from jax.experimental import pallas as pl
from jax.experimental.pallas import tpu as pltpu
from jax.sharding import PartitionSpec as P


BLK = 128
EXTRA = 8
SHIFT = 14.0
TINY = 1e-30
X = 4
MEMBERS = 4 * X
HALF = 2 * X


def swap_half(i):
    return i ^ HALF


def swap_core(i):
    return i ^ 1


def along_x(step):
    def move(i):
        return (i // HALF) * HALF + ((i // 2 + step) % X) * 2 + i % 2

    return move


def send(value, target):
    return lax.ppermute(value, "tensor", [(i, target(i)) for i in range(MEMBERS)])


def gather_rows(pieces, cols):
    return jnp.concatenate(
        [jnp.concatenate([piece[:, c] for piece in pieces], 0) for c in cols], 1
    )


def blocks_of(table_ref, slots):
    return [pl.ds(pl.multiple_of(table_ref[s] * BLK, BLK), BLK) for s in slots]


def weight_kernel(count, first, coded, rows_ref, cols_ref, offs_ref, *refs):
    pieces, hidden_ref, out_ref = refs[:count], refs[count], refs[-1]
    spans = [
        pl.ds(pl.multiple_of(offs_ref[first + i], 16), piece.shape[0])
        for i, piece in enumerate(pieces)
    ]

    def pair_step(pair, carry):
        slots = (2 * pair, 2 * pair + 1)
        grad = gather_rows(pieces, blocks_of(cols_ref, slots))
        act = jnp.concatenate(
            [
                jnp.concatenate([hidden_ref[span, r] for span in spans], 0)
                for r in blocks_of(rows_ref, slots)
            ],
            1,
        )
        blocks = lax.dot_general(
            act, grad, (((0,), (0,)), ((), ())), preferred_element_type=jnp.float32
        )
        for k, s in enumerate(slots):
            block = blocks[k * BLK : (k + 1) * BLK, k * BLK : (k + 1) * BLK]
            if coded:
                block = block + refs[count + 1][s]
                top = jnp.max(jnp.abs(block), axis=0, keepdims=True)
                power = jnp.ceil(jnp.log2(jnp.maximum(top, TINY)))
                out_ref[s, :BLK, :] = block * jnp.exp2(SHIFT - power)
                out_ref[s, BLK:, :] = jnp.broadcast_to(power, (EXTRA, BLK))
            else:
                out_ref[s] = block
        return carry

    lax.fori_loop(0, rows_ref.shape[0] // 2, pair_step, 0)


def input_kernel(count, rows_ref, cols_ref, offs_ref, counts_ref, *refs):
    pieces, (weights_ref, out_ref, total) = refs[:count], refs[count:]
    total[...] = jnp.zeros_like(total)
    nothing = jnp.zeros((BLK, BLK), weights_ref.dtype)

    def pair_step(pair, carry):
        slots = (2 * pair, 2 * pair + 1)
        grad = gather_rows(pieces, blocks_of(cols_ref, slots))
        w = []
        for s in slots:
            live = (s < counts_ref[0]).astype(jnp.float32)
            w.append((weights_ref[s].astype(jnp.float32) * live).astype(weights_ref.dtype))
        both = jnp.concatenate(
            [jnp.concatenate([w[0], nothing], 1), jnp.concatenate([nothing, w[1]], 1)], 0
        )
        moved = lax.dot_general(
            grad, both, (((1,), (1,)), ((), ())), preferred_element_type=jnp.float32
        )
        for k, r in enumerate(blocks_of(rows_ref, slots)):
            total[:, r] += moved[:, k * BLK : (k + 1) * BLK]
        return carry

    lax.fori_loop(0, rows_ref.shape[0] // 2, pair_step, 0)
    done = 0
    for i, piece in enumerate(pieces):
        height = piece.shape[0]
        span = pl.ds(pl.multiple_of(offs_ref[i], 16), height)
        out_ref[span, :] = total[done : done + height, :].astype(out_ref.dtype)
        done += height


def call(kernel, tables, operands, out, scratch, flops, grant):
    size = sum(v.size * v.dtype.itemsize for v in (*operands, out))
    held = pl.BlockSpec(memory_space=pltpu.VMEM)
    table = pl.BlockSpec(memory_space=pltpu.SMEM)
    return pl.pallas_call(
        kernel,
        in_specs=[table for _ in tables] + [held for _ in operands],
        out_specs=held,
        scratch_shapes=scratch,
        out_shape=out,
        compiler_params=pltpu.CompilerParams(vmem_limit_bytes=grant),
        cost_estimate=pl.CostEstimate(flops=flops, bytes_accessed=size, transcendentals=0),
    )(*tables, *operands)


def weight_grads(pieces, first, tables, hidden, slots, prior=None):
    coded = prior is not None
    kernel = functools.partial(weight_kernel, len(pieces), first, coded)
    out = jax.ShapeDtypeStruct((slots, BLK + EXTRA * coded, BLK), jnp.float32)
    operands = (*pieces, hidden) + ((prior,) if coded else ())
    flops = 2 * slots * sum(p.shape[0] for p in pieces) * BLK * BLK
    return call(kernel, tables, operands, out, [], flops, GRANT)


def input_grads(pieces, tables, weights, like):
    kernel = functools.partial(input_kernel, len(pieces))
    out = jax.ShapeDtypeStruct(like.shape, like.dtype)
    flops = 2 * weights.shape[0] * like.shape[0] * BLK * BLK
    scratch = [pltpu.VMEM(like.shape, jnp.float32)]
    return call(kernel, tables, (*pieces, weights), out, scratch, flops, 3 * GRANT)


def shards(hidden, out_grad, weights, block_rows, block_cols, counts):
    return body(hidden, out_grad, weights[0], block_rows[0], block_cols[0], counts)


def body(hidden, out_grad, weights, rows, cols, counts):
    height = out_grad.shape[0]
    slots = weights.shape[0]
    me = lax.axis_index("tensor")
    half, x, core = me // HALF, (me // 2) % X, me % 2

    other = send(out_grad, swap_half)
    parts = {}
    for side, own in (("near", out_grad), ("far", other)):
        parts[side, 0] = own
        parts[side, 1] = send(own, along_x(1))
        parts[side, X - 1] = send(own, along_x(X - 1))
    parts["near", 2] = send(parts["near", 1], along_x(1))
    parts["far", 2] = send(parts["far", 1][:CUT], along_x(1))
    parts["far", -2] = send(parts["far", X - 1][CUT:], along_x(X - 1))
    pieces, table = [], []
    for side, k in ORDER:
        shard = parts[side, k]
        pieces += [shard, send(shard, swap_core)]
        start = CUT if k == -2 else 0
        table += [(int(side == "far"), k % X, swapped, start) for swapped in (0, 1)]
    flip, step, swapped, start = (jnp.array(v, jnp.int32) for v in zip(*table))
    chip = (half ^ flip) * HALF + (x - step + X) % X * 2
    tables = (rows, cols, (chip + (core ^ swapped)) * height + start)

    prior = weight_grads(pieces[:EARLY], 0, tables, hidden, slots)
    coded = weight_grads(pieces[EARLY:], EARLY, tables, hidden, slots, prior)
    parts = lax.all_to_all(
        coded.astype(jnp.float16), "dp", split_axis=0, concat_axis=0, tiled=True
    )
    for i in range(EARLY, len(pieces), 2):
        shard, _ = lax.optimization_barrier((pieces[i], coded))
        pieces[i + 1] = send(shard, swap_core)
    input_grad = input_grads(pieces, (*tables, counts), weights, hidden)

    share = slots // lax.axis_size("dp")
    parts = parts.astype(jnp.float32).reshape(-1, share, BLK + EXTRA, BLK)
    summed = (parts[:, :, :BLK] * jnp.exp2(parts[:, :, BLK : BLK + 1] - SHIFT)).sum(0)
    mine = lax.axis_index("dp") * share + jnp.arange(share, dtype=jnp.int32)
    summed = jnp.where((mine < counts[0])[:, None, None], summed, 0.0)
    return summed[None], input_grad


ORDER = (
    ("near", 0), ("near", 1), ("near", X - 1), ("far", 0),
    ("near", 2), ("far", 1), ("far", X - 1), ("far", 2), ("far", -2),
)
EARLY = 8
CUT = 16
GRANT = 8 * 2**20


def solution(mesh):
    in_specs = (
        P("dp", "tensor"),
        P(("dp", "tensor"), None),
        P("tensor", None, None, None),
        P("tensor", None),
        P("tensor", None),
        P("tensor"),
    )
    out_specs = (P("tensor", "dp", None, None), P("dp", "tensor"))
    return jax.shard_map(
        shards, mesh=mesh, in_specs=in_specs, out_specs=out_specs, check_vma=False
    )
```

```python
import functools

import jax
import jax.numpy as jnp
from jax import lax
from jax.experimental import pallas as pl
from jax.experimental.pallas import tpu as pltpu
from jax.sharding import PartitionSpec as P


BLK = 128
EXTRA = 8
SHIFT = 14.0
TINY = 1e-30
X = 4
MEMBERS = 4 * X
HALF = 2 * X


def swap_half(i):
    return i ^ HALF


def swap_core(i):
    return i ^ 1


def along_x(step):
    def move(i):
        return (i // HALF) * HALF + ((i // 2 + step) % X) * 2 + i % 2

    return move


def send(value, target):
    return lax.ppermute(value, "tensor", [(i, target(i)) for i in range(MEMBERS)])


def gather_rows(pieces, cols):
    return jnp.concatenate(
        [jnp.concatenate([piece[:, c] for piece in pieces], 0) for c in cols], 1
    )


def blocks_of(cells_ref, wide, slots):
    cells = [cells_ref[s] for s in slots]
    rows = [pl.ds(pl.multiple_of(lax.div(c, wide) * BLK, BLK), BLK) for c in cells]
    cols = [pl.ds(pl.multiple_of(lax.rem(c, wide) * BLK, BLK), BLK) for c in cells]
    return rows, cols


def weight_kernel(count, first, coded, cells_ref, offs_ref, *refs):
    pieces, hidden_ref, out_ref = refs[:count], refs[count], refs[-1]
    spans = [
        pl.ds(pl.multiple_of(offs_ref[first + i], 16), piece.shape[0])
        for i, piece in enumerate(pieces)
    ]

    def pair_step(pair, carry):
        slots = (2 * pair, 2 * pair + 1)
        rows, cols = blocks_of(cells_ref, pieces[0].shape[1] // BLK, slots)
        grad = gather_rows(pieces, cols)
        act = jnp.concatenate(
            [
                jnp.concatenate([hidden_ref[span, r] for span in spans], 0)
                for r in rows
            ],
            1,
        )
        blocks = lax.dot_general(
            act, grad, (((0,), (0,)), ((), ())), preferred_element_type=jnp.float32
        )
        for k, s in enumerate(slots):
            block = blocks[k * BLK : (k + 1) * BLK, k * BLK : (k + 1) * BLK]
            if coded:
                block = block + refs[count + 1][s]
                top = jnp.max(jnp.abs(block), axis=0, keepdims=True)
                power = jnp.ceil(jnp.log2(jnp.maximum(top, TINY)))
                out_ref[s, :BLK, :] = block * jnp.exp2(SHIFT - power)
                out_ref[s, BLK:, :] = jnp.broadcast_to(power, (EXTRA, BLK))
            else:
                out_ref[s] = block
        return carry

    lax.fori_loop(0, cells_ref.shape[0] // 2, pair_step, 0)


def input_kernel(count, cells_ref, offs_ref, counts_ref, *refs):
    pieces, (weights_ref, out_ref, total) = refs[:count], refs[count:]
    total[...] = jnp.zeros_like(total)
    nothing = jnp.zeros((BLK, BLK), weights_ref.dtype)

    def pair_step(pair, carry):
        slots = (2 * pair, 2 * pair + 1)
        rows, cols = blocks_of(cells_ref, pieces[0].shape[1] // BLK, slots)
        grad = gather_rows(pieces, cols)
        w = []
        for s in slots:
            live = (s < counts_ref[0]).astype(jnp.float32)
            w.append((weights_ref[s].astype(jnp.float32) * live).astype(weights_ref.dtype))
        both = jnp.concatenate(
            [jnp.concatenate([w[0], nothing], 1), jnp.concatenate([nothing, w[1]], 1)], 0
        )
        moved = lax.dot_general(
            grad, both, (((1,), (1,)), ((), ())), preferred_element_type=jnp.float32
        )
        for k, r in enumerate(rows):
            total[:, r] += moved[:, k * BLK : (k + 1) * BLK]
        return carry

    lax.fori_loop(0, cells_ref.shape[0] // 2, pair_step, 0)
    done = 0
    for i, piece in enumerate(pieces):
        height = piece.shape[0]
        span = pl.ds(pl.multiple_of(offs_ref[i], 16), height)
        out_ref[span, :] = total[done : done + height, :].astype(out_ref.dtype)
        done += height


def call(kernel, tables, operands, out, scratch, flops, grant):
    size = sum(v.size * v.dtype.itemsize for v in (*operands, out))
    held = pl.BlockSpec(memory_space=pltpu.VMEM)
    table = pl.BlockSpec(memory_space=pltpu.SMEM)
    return pl.pallas_call(
        kernel,
        in_specs=[table for _ in tables] + [held for _ in operands],
        out_specs=held,
        scratch_shapes=scratch,
        out_shape=out,
        compiler_params=pltpu.CompilerParams(vmem_limit_bytes=grant),
        cost_estimate=pl.CostEstimate(flops=flops, bytes_accessed=size, transcendentals=0),
    )(*tables, *operands)


def weight_grads(pieces, first, tables, hidden, slots, prior=None):
    coded = prior is not None
    kernel = functools.partial(weight_kernel, len(pieces), first, coded)
    out = jax.ShapeDtypeStruct((slots, BLK + EXTRA * coded, BLK), jnp.float32)
    operands = (*pieces, hidden) + ((prior,) if coded else ())
    flops = 2 * slots * sum(p.shape[0] for p in pieces) * BLK * BLK
    return call(kernel, tables, operands, out, [], flops, GRANT)


def input_grads(pieces, tables, weights, like):
    kernel = functools.partial(input_kernel, len(pieces))
    out = jax.ShapeDtypeStruct(like.shape, like.dtype)
    flops = 2 * weights.shape[0] * like.shape[0] * BLK * BLK
    scratch = [pltpu.VMEM(like.shape, jnp.float32)]
    return call(kernel, tables, (*pieces, weights), out, scratch, flops, 3 * GRANT)


def shards(hidden, out_grad, weights, block_rows, block_cols, counts):
    return body(hidden, out_grad, weights[0], block_rows[0], block_cols[0], counts)


def body(hidden, out_grad, weights, rows, cols, counts):
    height = out_grad.shape[0]
    slots = weights.shape[0]
    me = lax.axis_index("tensor")
    half, x, core = me // HALF, (me // 2) % X, me % 2

    other = send(out_grad, swap_half)
    parts = {}
    for side, own in (("near", out_grad), ("far", other)):
        parts[side, 0] = own
        parts[side, 1] = send(own, along_x(1))
        parts[side, X - 1] = send(own, along_x(X - 1))
    parts["near", 2] = send(parts["near", 1], along_x(1))
    parts["far", 2] = send(parts["far", 1][:CUT], along_x(1))
    parts["far", -2] = send(parts["far", X - 1][CUT:], along_x(X - 1))
    pieces, table = [], []
    for side, k in ORDER:
        shard = parts[side, k]
        pieces += [shard, send(shard, swap_core)]
        start = CUT if k == -2 else 0
        table += [(int(side == "far"), k % X, swapped, start) for swapped in (0, 1)]
    flip, step, swapped, start = (jnp.array(v, jnp.int32) for v in zip(*table))
    chip = (half ^ flip) * HALF + (x - step + X) % X * 2
    cells = rows * (out_grad.shape[1] // BLK) + cols
    tables = (cells, (chip + (core ^ swapped)) * height + start)

    prior = weight_grads(pieces[:EARLY], 0, tables, hidden, slots)
    coded = weight_grads(pieces[EARLY:], EARLY, tables, hidden, slots, prior)
    parts = lax.all_to_all(
        coded.astype(jnp.float16), "dp", split_axis=0, concat_axis=0, tiled=True
    )
    for i in range(EARLY, len(pieces), 2):
        shard, _ = lax.optimization_barrier((pieces[i], coded))
        pieces[i + 1] = send(shard, swap_core)
    input_grad = input_grads(pieces, (*tables, counts), weights, hidden)

    share = slots // lax.axis_size("dp")
    values = parts[:, :BLK].astype(jnp.float32)
    powers = parts[:, BLK : BLK + 1].astype(jnp.float32)
    summed = (values * jnp.exp2(powers - SHIFT)).reshape(-1, share, BLK, BLK).sum(0)
    mine = lax.axis_index("dp") * share + jnp.arange(share, dtype=jnp.int32)
    summed = jnp.where((mine < counts[0])[:, None, None], summed, 0.0)
    return summed[None], input_grad


ORDER = (
    ("near", 0), ("near", 1), ("near", X - 1),
    ("near", 2), ("far", 0), ("far", 1), ("far", X - 1), ("far", 2), ("far", -2),
)
EARLY = 6
CUT = 16
GRANT = 8 * 2**20


def solution(mesh):
    in_specs = (
        P("dp", "tensor"),
        P(("dp", "tensor"), None),
        P("tensor", None, None, None),
        P("tensor", None),
        P("tensor", None),
        P("tensor"),
    )
    out_specs = (P("tensor", "dp", None, None), P("dp", "tensor"))
    return jax.shard_map(
        shards, mesh=mesh, in_specs=in_specs, out_specs=out_specs, check_vma=False
    )
```

```python
import functools

import jax
import jax.numpy as jnp
from jax import lax
from jax.experimental import pallas as pl
from jax.experimental.pallas import tpu as pltpu
from jax.sharding import PartitionSpec as P


BLK = 128
EXTRA = 8
SHIFT = 14.0
TINY = 1e-30
X = 4
MEMBERS = 4 * X
HALF = 2 * X


def swap_half(i):
    return i ^ HALF


def swap_core(i):
    return i ^ 1


def along_x(step):
    def move(i):
        return (i // HALF) * HALF + ((i // 2 + step) % X) * 2 + i % 2

    return move


def send(value, target):
    return lax.ppermute(value, "tensor", [(i, target(i)) for i in range(MEMBERS)])


def gather_rows(pieces, cols):
    return jnp.concatenate(
        [jnp.concatenate([piece[:, c] for piece in pieces], 0) for c in cols], 1
    )


def blocks_of(cells_ref, wide, slots):
    cells = [cells_ref[s] for s in slots]
    rows = [pl.ds(pl.multiple_of(lax.div(c, wide) * BLK, BLK), BLK) for c in cells]
    cols = [pl.ds(pl.multiple_of(lax.rem(c, wide) * BLK, BLK), BLK) for c in cells]
    return rows, cols


def weight_kernel(count, first, prior, coded, cells_ref, offs_ref, *refs):
    pieces, hidden_ref, out_ref = refs[:count], refs[count], refs[-1]
    spans = [
        pl.ds(pl.multiple_of(offs_ref[first + i], 16), piece.shape[0])
        for i, piece in enumerate(pieces)
    ]

    def pair_step(pair, carry):
        slots = (2 * pair, 2 * pair + 1)
        rows, cols = blocks_of(cells_ref, pieces[0].shape[1] // BLK, slots)
        grad = gather_rows(pieces, cols)
        act = jnp.concatenate(
            [
                jnp.concatenate([hidden_ref[span, r] for span in spans], 0)
                for r in rows
            ],
            1,
        )
        blocks = lax.dot_general(
            act, grad, (((0,), (0,)), ((), ())), preferred_element_type=jnp.float32
        )
        for k, s in enumerate(slots):
            block = blocks[k * BLK : (k + 1) * BLK, k * BLK : (k + 1) * BLK]
            if prior:
                block = block + refs[count + 1][s]
            if coded:
                top = jnp.max(jnp.abs(block), axis=0, keepdims=True)
                power = jnp.ceil(jnp.log2(jnp.maximum(top, TINY)))
                out_ref[s, :BLK, :] = block * jnp.exp2(SHIFT - power)
                out_ref[s, BLK:, :] = jnp.broadcast_to(power, (EXTRA, BLK))
            else:
                out_ref[s] = block
        return carry

    lax.fori_loop(0, cells_ref.shape[0] // 2, pair_step, 0)


def input_kernel(count, cells_ref, offs_ref, counts_ref, *refs):
    pieces, (weights_ref, out_ref, total) = refs[:count], refs[count:]
    total[...] = jnp.zeros_like(total)
    nothing = jnp.zeros((BLK, BLK), weights_ref.dtype)

    def pair_step(pair, carry):
        slots = (2 * pair, 2 * pair + 1)
        rows, cols = blocks_of(cells_ref, pieces[0].shape[1] // BLK, slots)
        grad = gather_rows(pieces, cols)
        w = []
        for s in slots:
            live = (s < counts_ref[0]).astype(jnp.float32)
            w.append((weights_ref[s].astype(jnp.float32) * live).astype(weights_ref.dtype))
        both = jnp.concatenate(
            [jnp.concatenate([w[0], nothing], 1), jnp.concatenate([nothing, w[1]], 1)], 0
        )
        moved = lax.dot_general(
            grad, both, (((1,), (1,)), ((), ())), preferred_element_type=jnp.float32
        )
        for k, r in enumerate(rows):
            total[:, r] += moved[:, k * BLK : (k + 1) * BLK]
        return carry

    lax.fori_loop(0, cells_ref.shape[0] // 2, pair_step, 0)
    done = 0
    for i, piece in enumerate(pieces):
        height = piece.shape[0]
        span = pl.ds(pl.multiple_of(offs_ref[i], 16), height)
        out_ref[span, :] = total[done : done + height, :].astype(out_ref.dtype)
        done += height


def call(kernel, tables, operands, out, scratch, flops, grant):
    size = sum(v.size * v.dtype.itemsize for v in (*operands, out))
    held = pl.BlockSpec(memory_space=pltpu.VMEM)
    table = pl.BlockSpec(memory_space=pltpu.SMEM)
    return pl.pallas_call(
        kernel,
        in_specs=[table for _ in tables] + [held for _ in operands],
        out_specs=held,
        scratch_shapes=scratch,
        out_shape=out,
        compiler_params=pltpu.CompilerParams(vmem_limit_bytes=grant),
        cost_estimate=pl.CostEstimate(flops=flops, bytes_accessed=size, transcendentals=0),
    )(*tables, *operands)


def weight_grads(pieces, first, tables, hidden, slots, prior=None, coded=False):
    kernel = functools.partial(weight_kernel, len(pieces), first, prior is not None, coded)
    out = jax.ShapeDtypeStruct((slots, BLK + EXTRA * coded, BLK), jnp.float32)
    operands = (*pieces, hidden) + (() if prior is None else (prior,))
    flops = 2 * slots * sum(p.shape[0] for p in pieces) * BLK * BLK
    return call(kernel, tables, operands, out, [], flops, GRANT)


def input_grads(pieces, tables, weights, like):
    kernel = functools.partial(input_kernel, len(pieces))
    out = jax.ShapeDtypeStruct(like.shape, like.dtype)
    flops = 2 * weights.shape[0] * like.shape[0] * BLK * BLK
    scratch = [pltpu.VMEM(like.shape, jnp.float32)]
    return call(kernel, tables, (*pieces, weights), out, scratch, flops, 3 * GRANT)


def shards(hidden, out_grad, weights, block_rows, block_cols, counts):
    return body(hidden, out_grad, weights[0], block_rows[0], block_cols[0], counts)


def body(hidden, out_grad, weights, rows, cols, counts):
    height = out_grad.shape[0]
    slots = weights.shape[0]
    me = lax.axis_index("tensor")
    half, x, core = me // HALF, (me // 2) % X, me % 2

    other = send(out_grad, swap_half)
    parts = {}
    for side, own in (("near", out_grad), ("far", other)):
        parts[side, 0] = own
        parts[side, 1] = send(own, along_x(1))
        parts[side, X - 1] = send(own, along_x(X - 1))
    parts["near", 2] = send(parts["near", 1], along_x(1))
    parts["far", 2] = send(parts["far", 1][:CUT], along_x(1))
    parts["far", -2] = send(parts["far", X - 1][CUT:], along_x(X - 1))
    pieces, table = [], []
    for side, k in ORDER:
        shard = parts[side, k]
        pieces += [shard, send(shard, swap_core)]
        start = CUT if k == -2 else 0
        table += [(int(side == "far"), k % X, swapped, start) for swapped in (0, 1)]
    flip, step, swapped, start = (jnp.array(v, jnp.int32) for v in zip(*table))
    chip = (half ^ flip) * HALF + (x - step + X) % X * 2
    cells = rows * (out_grad.shape[1] // BLK) + cols
    tables = (cells, (chip + (core ^ swapped)) * height + start)

    prior = weight_grads(pieces[:EARLY], 0, tables, hidden, slots)
    prior = weight_grads(pieces[EARLY:LATE], EARLY, tables, hidden, slots, prior)
    coded = weight_grads(pieces[LATE:], LATE, tables, hidden, slots, prior, coded=True)
    parts = lax.all_to_all(coded.astype(jnp.float16), "dp", split_axis=0, concat_axis=0, tiled=True)
    for i in range(AGAIN, len(pieces), 2):
        shard, _ = lax.optimization_barrier((pieces[i], coded))
        pieces[i + 1] = send(shard, swap_core)
    input_grad = input_grads(pieces, (*tables, counts), weights, hidden)

    share = slots // lax.axis_size("dp")
    parts = parts.astype(jnp.float32).reshape(-1, share, BLK + EXTRA, BLK)
    summed = (parts[:, :, :BLK] * jnp.exp2(parts[:, :, BLK : BLK + 1] - SHIFT)).sum(0)
    mine = lax.axis_index("dp") * share + jnp.arange(share, dtype=jnp.int32)
    summed = jnp.where((mine < counts[0])[:, None, None], summed, 0.0)
    return summed[None], input_grad


ORDER = (
    ("near", 0), ("near", 1), ("near", X - 1),
    ("near", 2), ("far", 0), ("far", 1), ("far", X - 1), ("far", 2), ("far", -2),
)
EARLY = 6
LATE = 14
AGAIN = 10
CUT = 16
GRANT = 8 * 2**20


def solution(mesh):
    in_specs = (
        P("dp", "tensor"),
        P(("dp", "tensor"), None),
        P("tensor", None, None, None),
        P("tensor", None),
        P("tensor", None),
        P("tensor"),
    )
    out_specs = (P("tensor", "dp", None, None), P("dp", "tensor"))
    return jax.shard_map(
        shards, mesh=mesh, in_specs=in_specs, out_specs=out_specs, check_vma=False
    )
```

```python
import functools

import jax
import jax.numpy as jnp
from jax import lax
from jax.experimental import pallas as pl
from jax.experimental.pallas import tpu as pltpu
from jax.sharding import PartitionSpec as P


BLK = 128
EXTRA = 8
SHIFT = 14.0
TINY = 1e-30
X = 4
MEMBERS = 4 * X
HALF = 2 * X


def swap_half(i):
    return i ^ HALF


def swap_core(i):
    return i ^ 1


def along_x(step):
    def move(i):
        return (i // HALF) * HALF + ((i // 2 + step) % X) * 2 + i % 2

    return move


def send(value, target):
    return lax.ppermute(value, "tensor", [(i, target(i)) for i in range(MEMBERS)])


def gather_rows(pieces, cols):
    return jnp.concatenate(
        [jnp.concatenate([piece[:, c] for piece in pieces], 0) for c in cols], 1
    )


def blocks_of(cells_ref, wide, slots):
    cells = [cells_ref[s] for s in slots]
    rows = [pl.ds(pl.multiple_of(lax.div(c, wide) * BLK, BLK), BLK) for c in cells]
    cols = [pl.ds(pl.multiple_of(lax.rem(c, wide) * BLK, BLK), BLK) for c in cells]
    return rows, cols


def weight_kernel(count, first, coded, cells_ref, offs_ref, *refs):
    pieces, hidden_ref, out_ref = refs[:count], refs[count], refs[-1]
    spans = [
        pl.ds(pl.multiple_of(offs_ref[first + i], 16), piece.shape[0])
        for i, piece in enumerate(pieces)
    ]

    def pair_step(pair, carry):
        slots = (2 * pair, 2 * pair + 1)
        rows, cols = blocks_of(cells_ref, pieces[0].shape[1] // BLK, slots)
        grad = gather_rows(pieces, cols)
        act = jnp.concatenate(
            [
                jnp.concatenate([hidden_ref[span, r] for span in spans], 0)
                for r in rows
            ],
            1,
        )
        blocks = lax.dot_general(
            act, grad, (((0,), (0,)), ((), ())), preferred_element_type=jnp.float32
        )
        for k, s in enumerate(slots):
            block = blocks[k * BLK : (k + 1) * BLK, k * BLK : (k + 1) * BLK]
            if coded:
                block = block + refs[count + 1][s]
                top = jnp.max(jnp.abs(block), axis=0, keepdims=True)
                power = jnp.ceil(jnp.log2(jnp.maximum(top, TINY)))
                out_ref[s, :BLK, :] = block * jnp.exp2(SHIFT - power)
                out_ref[s, BLK:, :] = jnp.broadcast_to(power, (EXTRA, BLK))
            else:
                out_ref[s] = block
        return carry

    lax.fori_loop(0, cells_ref.shape[0] // 2, pair_step, 0)


def input_kernel(count, cells_ref, offs_ref, counts_ref, *refs):
    pieces, (weights_ref, out_ref, total) = refs[:count], refs[count:]
    total[...] = jnp.zeros_like(total)
    nothing = jnp.zeros((BLK, BLK), weights_ref.dtype)

    def pair_step(pair, carry):
        slots = (2 * pair, 2 * pair + 1)
        rows, cols = blocks_of(cells_ref, pieces[0].shape[1] // BLK, slots)
        grad = gather_rows(pieces, cols)
        w = []
        for s in slots:
            live = (s < counts_ref[0]).astype(jnp.float32)
            w.append((weights_ref[s].astype(jnp.float32) * live).astype(weights_ref.dtype))
        both = jnp.concatenate(
            [jnp.concatenate([w[0], nothing], 1), jnp.concatenate([nothing, w[1]], 1)], 0
        )
        moved = lax.dot_general(
            grad, both, (((1,), (1,)), ((), ())), preferred_element_type=jnp.float32
        )
        for k, r in enumerate(rows):
            total[:, r] += moved[:, k * BLK : (k + 1) * BLK]
        return carry

    lax.fori_loop(0, cells_ref.shape[0] // 2, pair_step, 0)
    done = 0
    for i, piece in enumerate(pieces):
        height = piece.shape[0]
        span = pl.ds(pl.multiple_of(offs_ref[i], 16), height)
        out_ref[span, :] = total[done : done + height, :].astype(out_ref.dtype)
        done += height


def call(kernel, tables, operands, out, scratch, flops, grant):
    size = sum(v.size * v.dtype.itemsize for v in (*operands, out))
    held = pl.BlockSpec(memory_space=pltpu.VMEM)
    table = pl.BlockSpec(memory_space=pltpu.SMEM)
    return pl.pallas_call(
        kernel,
        in_specs=[table for _ in tables] + [held for _ in operands],
        out_specs=held,
        scratch_shapes=scratch,
        out_shape=out,
        compiler_params=pltpu.CompilerParams(vmem_limit_bytes=grant),
        cost_estimate=pl.CostEstimate(flops=flops, bytes_accessed=size, transcendentals=0),
    )(*tables, *operands)


def weight_grads(pieces, first, tables, hidden, slots, prior=None):
    coded = prior is not None
    kernel = functools.partial(weight_kernel, len(pieces), first, coded)
    out = jax.ShapeDtypeStruct((slots, BLK + EXTRA * coded, BLK), jnp.float32)
    operands = (*pieces, hidden) + ((prior,) if coded else ())
    flops = 2 * slots * sum(p.shape[0] for p in pieces) * BLK * BLK
    return call(kernel, tables, operands, out, [], flops, GRANT)


def input_grads(pieces, tables, weights, like):
    kernel = functools.partial(input_kernel, len(pieces))
    out = jax.ShapeDtypeStruct(like.shape, like.dtype)
    flops = 2 * weights.shape[0] * like.shape[0] * BLK * BLK
    scratch = [pltpu.VMEM(like.shape, jnp.float32)]
    return call(kernel, tables, (*pieces, weights), out, scratch, flops, 3 * GRANT)


def shards(hidden, out_grad, weights, block_rows, block_cols, counts):
    return body(hidden, out_grad, weights[0], block_rows[0], block_cols[0], counts)


def body(hidden, out_grad, weights, rows, cols, counts):
    height = out_grad.shape[0]
    slots = weights.shape[0]
    me = lax.axis_index("tensor")
    half, x, core = me // HALF, (me // 2) % X, me % 2

    other = send(out_grad, swap_half)
    parts = {}
    for side, own in (("near", out_grad), ("far", other)):
        parts[side, 0] = own
        parts[side, 1] = send(own, along_x(1))
        parts[side, X - 1] = send(own, along_x(X - 1))
    parts["near", 2] = send(parts["near", 1], along_x(1))
    parts["far", 2] = send(parts["far", 1][:CUT], along_x(1))
    parts["far", -2] = send(parts["far", X - 1][CUT:], along_x(X - 1))
    pieces, table = [], []
    for side, k in ORDER:
        shard = parts[side, k]
        pieces += [shard, send(shard, swap_core)]
        start = CUT if k == -2 else 0
        table += [(int(side == "far"), k % X, swapped, start) for swapped in (0, 1)]
    flip, step, swapped, start = (jnp.array(v, jnp.int32) for v in zip(*table))
    chip = (half ^ flip) * HALF + (x - step + X) % X * 2
    cells = rows * (out_grad.shape[1] // BLK) + cols
    tables = (cells, (chip + (core ^ swapped)) * height + start)

    prior = weight_grads(pieces[:EARLY], 0, tables, hidden, slots)
    coded = weight_grads(pieces[EARLY:], EARLY, tables, hidden, slots, prior)
    parts = lax.all_to_all(
        coded.astype(jnp.float16), "dp", split_axis=0, concat_axis=0, tiled=True
    )
    for i in range(EARLY, len(pieces), 2):
        shard, _ = lax.optimization_barrier((pieces[i], coded))
        pieces[i + 1] = send(shard, swap_core)
    input_grad = input_grads(pieces, (*tables, counts), weights, hidden)

    share = slots // lax.axis_size("dp")
    parts = parts.astype(jnp.float32).reshape(-1, share, BLK + EXTRA, BLK)
    summed = (parts[:, :, :BLK] * jnp.exp2(parts[:, :, BLK : BLK + 1] - SHIFT)).sum(0)
    mine = lax.axis_index("dp") * share + jnp.arange(share, dtype=jnp.int32)
    summed = jnp.where((mine < counts[0])[:, None, None], summed, 0.0)
    return summed[None], input_grad


ORDER = (
    ("near", 0), ("near", 1), ("near", X - 1), ("far", 0),
    ("near", 2), ("far", 1), ("far", X - 1), ("far", 2), ("far", -2),
)
EARLY = 8
CUT = 16
GRANT = 8 * 2**20


def solution(mesh):
    in_specs = (
        P("dp", "tensor"),
        P(("dp", "tensor"), None),
        P("tensor", None, None, None),
        P("tensor", None),
        P("tensor", None),
        P("tensor"),
    )
    out_specs = (P("tensor", "dp", None, None), P("dp", "tensor"))
    return jax.shard_map(
        shards, mesh=mesh, in_specs=in_specs, out_specs=out_specs, check_vma=False
    )
```
